256 devices in a mesh: seq: 32 (over x, y, core), head: 8 (over z).
Axes of the slice: x: 4, y: 4, z: 8, core: 2. Of those that a mesh axis runs over, the one named last changes fastest.
Arguments:
- queries: bfloat16 [24576, 8192], P('seq', 'head'), may hold values from -140 to 140
- key_weight: bfloat16 [1024, 8192], P(None, 'head'), may hold values from -0.1875 to 0.1875
- value_weight: bfloat16 [1024, 8192], P(None, 'head'), may hold values from -0.1875 to 0.1875
- encodings: bfloat16 [256, 128, 1024], P('seq', None, 'head'), may hold values from -6 to 6
- nb_owner: int32 [384, 2], P('seq'), may hold values from 0 to 31, all different within a row; in each aligned block of 12 rows (0 to 11, 12 to 23, ...) at most 2 rows name the same one
- nb_block: int32 [384, 2], P('seq'), may hold values from 0 to 7
Outputs:
- attended: bfloat16 [24576, 8192], P('seq', 'head')
The draws below stay inside these ranges and needn't reach their ends.
Inputs may be any that keep to these rules, and one draw needn't show every extreme that they name: `nb_owner`: the 2 neighbours of a span have different owners. Among the spans of one device no owner is named more than 2 times, and in every draw some device names some owner exactly 2 times.
All inputs are finite; a program needn't handle non-finite values.
Results may differ from the reference program's by a relative error of at most 0.012.
The reference program's roundings to bfloat16 on the way count: a program that leaves them out, or rounds other values in their place, can miss the bound.
Values may be sent and summed in bfloat16 or wider, within the bound.
A program may use at most 128 MiB of HBM per device.

```python
import math
import jax
import jax.numpy as jnp
import numpy as np
from jax import lax

HEADS = 64
HEAD_DIM = 128
ENC = 1024
SPAN = 64
NLEN = 128
NEIGH = 2
TOK_DEV = 768
DB_DEV = 8
CAP = 2
TOKENS = 24576
SPANS = 384
DB_BLOCKS = 256
N_SEQ = 32
N_HEAD = 8


def draw_queries(key, part):
    base_key = jax.random.fold_in(key, 0)
    array_shape = (TOKENS, HEADS * HEAD_DIM)
    return jnp.clip(jax.random.normal(base_key, array_shape, jnp.float32), -6.0, 6.0).astype(jnp.bfloat16)


def with_ends(values, key, smallest, top_value):
    spot = [jax.random.randint(jax.random.fold_in(key, axis), (), 0, length) for axis, length in enumerate(values.shape)]
    longest = values.shape.index(max(values.shape))
    neighbour = spot[:longest] + [(spot[longest] + 1) % values.shape[longest]] + spot[longest + 1:]
    return values.at[tuple(spot)].set(smallest).at[tuple(neighbour)].set(top_value)


def shard_levels(stream_key, dims, cuts, least, largest):
    factor_of = 1.0
    for position, shards_of in cuts:
        draws = jax.random.uniform(jax.random.fold_in(jax.random.fold_in(stream_key, 6), position), (shards_of,), jnp.float32, least / len(cuts), largest / len(cuts))
        factor_of = factor_of * jnp.repeat(jnp.exp(draws), dims[position] // shards_of).reshape((-1,) + (1,) * (len(dims) - 1 - position))
    return factor_of


def shared_out(own_key, own, number, rows, count, top, most, slope):
    order = jax.random.permutation(own_key, count)
    heavy_load, usual = portions_of(count, rows * top, most, slope, True), portions_of(count, rows * top, most, slope, False)
    places = jnp.arange(count)

    def named(lengths, rotation):
        used = int((lengths > 0).sum())
        fixed = max(1, used // 4)
        shifted = fixed + (places - fixed + rotation * (used - fixed)) % max(1, count - fixed)
        return jnp.zeros((count,), jnp.int32).at[order[jnp.where(places < fixed, places, shifted)]].set(jnp.asarray(lengths, jnp.int32))

    lengths = jnp.where(number % 4 == 0, named(heavy_load, number // 4), named(usual, number - number // 4 - 1))
    mixed = jax.random.permutation(jax.random.fold_in(own, 3), count)
    donor, sink = mixed[0:count // 2 * 2:2], mixed[1:count // 2 * 2:2]
    room = jnp.minimum(lengths[donor] - 1, most - lengths[sink]) // 2
    room = jnp.where((donor == order[0]) | (sink == order[0]) | (lengths[sink] == 0), 0, jnp.maximum(room, 0))
    shifted = jax.random.randint(jax.random.fold_in(own, 4), (count // 2,), 0, 1 << 20) % (room + 1)
    lengths = lengths.at[donor].add(-shifted).at[sink].add(shifted)
    items = jnp.searchsorted(jnp.cumsum(lengths), jnp.arange(rows * top), side="right").astype(jnp.int32)
    grid = items.reshape(top, rows).T
    grid = grid[jax.random.permutation(jax.random.fold_in(own, 1), rows)]
    rotation = jax.random.randint(jax.random.fold_in(own, 2), (rows, 1), 0, top)
    return jnp.take_along_axis(grid, (jnp.arange(top)[None, :] + rotation) % top, axis=1)


def portions_of(count, total, bound, skew, full):
    weights = [(1 << 20) // math.isqrt(standing ** skew) + 1 for standing in range(1, count + 1)]
    largest = bound if full else min(bound, max(-(-total // count), total * weights[0] // sum(weights)))
    least = 1 if total - largest >= count - 1 else 0
    counts, rest = [largest] + [least] * (count - 1), total - largest - least * (count - 1)
    while rest > 0:
        candidates = [i for i in range(1, count) if counts[i] < largest] or [i for i in range(1, count) if counts[i] < bound]
        whole, left = sum([weights[i] for i in candidates]), rest
        for i in candidates:
            extra = min(bound - counts[i], max(1, left * weights[i] // whole), rest)
            counts[i] = counts[i] + extra
            rest = rest - extra
    return np.array(counts)


def normal_values(key, extent, scale, bound, shards=(), kind=jnp.bfloat16):
    factor_of = shard_levels(key, extent, shards, -0.22, 0.18) if shards else 1.0
    values = jax.random.normal(key, extent, jnp.float32) * scale * factor_of
    return jnp.minimum(jnp.maximum(values, -bound), bound).astype(kind)


def setup_inputs(seed: int = 0) -> dict:
    seeds = jax.random.split(jax.random.key(seed), 7)
    queries = draw_queries(jax.random.fold_in(seeds[6], 71), 0)
    key_weight = normal_values(seeds[1], (ENC, HEADS * HEAD_DIM), ENC ** -0.5, 0.1875, ((1, 8),))
    value_weight = normal_values(seeds[2], (ENC, HEADS * HEAD_DIM), ENC ** -0.5, 0.1875, ((1, 8),))
    encodings = normal_values(seeds[3], (DB_BLOCKS, NLEN, ENC), 1.0, 6.0, ((0, 32), (2, 8)))
    nb_owner_keys = jax.random.split(jax.random.fold_in(seeds[4], 1), SPANS // (TOK_DEV // SPAN))
    nb_owner_turns = jax.random.permutation(jax.random.fold_in(seeds[4], 3), SPANS // (TOK_DEV // SPAN))
    nb_owner = jax.vmap(lambda own, number: shared_out(jax.random.fold_in(seeds[4], 2), own, number, TOK_DEV // SPAN, N_SEQ, NEIGH, CAP, 2))(nb_owner_keys, nb_owner_turns).reshape((SPANS, NEIGH))
    nb_block = with_ends(jax.random.randint(seeds[5], (SPANS, NEIGH), 0, DB_DEV), jax.random.fold_in(seeds[5], 1), 0, DB_DEV - 1).astype(jnp.int32)
    return {"queries": queries, "key_weight": key_weight, "value_weight": value_weight, "encodings": encodings, "nb_owner": nb_owner, "nb_block": nb_block}


def reference(queries, key_weight, value_weight, encodings, nb_owner, nb_block):
    block_ids = (nb_owner * DB_DEV + nb_block).astype(jnp.int32)
    flat_rows = encodings.reshape(DB_BLOCKS * NLEN, ENC)
    group_heads = HEADS // N_HEAD
    group_width = group_heads * HEAD_DIM
    inverse_root = 1.0 / math.sqrt(HEAD_DIM)

    def one_group(group_index):
        col_start = (group_index * group_width).astype(jnp.int32)
        key_cols = lax.dynamic_slice_in_dim(key_weight, col_start, group_width, 1)
        value_cols = lax.dynamic_slice_in_dim(value_weight, col_start, group_width, 1)
        key_table = jnp.dot(flat_rows, key_cols, preferred_element_type=jnp.float32).astype(jnp.bfloat16)
        value_table = jnp.dot(flat_rows, value_cols, preferred_element_type=jnp.float32).astype(jnp.bfloat16)
        key_table = key_table.reshape(DB_BLOCKS, NLEN, group_width)
        value_table = value_table.reshape(DB_BLOCKS, NLEN, group_width)
        span_keys = jnp.take(key_table, block_ids, axis=0).reshape(SPANS, NEIGH * NLEN, group_heads, HEAD_DIM)
        span_values = jnp.take(value_table, block_ids, axis=0).reshape(SPANS, NEIGH * NLEN, group_heads, HEAD_DIM)
        empty_span = jnp.zeros((1, NEIGH * NLEN, group_heads, HEAD_DIM), jnp.bfloat16)
        span_keys = jnp.concatenate([empty_span, span_keys], axis=0)
        span_values = jnp.concatenate([empty_span, span_values], axis=0)
        query_cols = lax.dynamic_slice_in_dim(queries, col_start, group_width, 1)
        grouped = jnp.pad(query_cols, ((1, SPAN - 1), (0, 0))).reshape(SPANS + 1, SPAN, group_heads, HEAD_DIM)
        scores = jnp.einsum('cqhd,ckhd->chqk', grouped.astype(jnp.float32), span_keys.astype(jnp.float32)) * inverse_root
        weights = jax.nn.softmax(scores, axis=-1).astype(jnp.bfloat16)
        attended = jnp.einsum('chqk,ckhd->cqhd', weights.astype(jnp.float32), span_values.astype(jnp.float32))
        attended = attended.reshape((SPANS + 1) * SPAN, group_width)[1:TOKENS + 1]
        return attended.astype(jnp.bfloat16)
    groups = lax.map(one_group, jnp.arange(N_HEAD, dtype=jnp.int32))
    return jnp.transpose(groups, (1, 0, 2)).reshape(TOKENS, HEADS * HEAD_DIM)
```

```python
import math

import jax
import jax.numpy as jnp
from jax import lax
from jax.experimental import pallas as pl
from jax.experimental.pallas import tpu as pltpu
from jax.sharding import PartitionSpec as P

HEAD_DIM = 128
SPAN = 64
CHUNK_SPANS = 2


def moved(shard, axis, by):
    devices = lax.axis_size(axis)
    pairs = [(i, i + by) for i in range(devices) if 0 <= i + by < devices]
    return lax.ppermute(shard, axis, pairs)


def project(x, wk_ref, wv_ref, kv):
    width = wk_ref.shape[1]
    for base, w_ref in ((0, wk_ref), (width, wv_ref)):

        @pl.loop(0, width // 256)
        def _(n):
            src = pl.ds(pl.multiple_of(n * 256, 256), 256)
            dst = pl.ds(pl.multiple_of(base + n * 256, 256), 256)
            kv[:, dst] = jnp.dot(
                x[...], w_ref[:, src], preferred_element_type=jnp.float32
            ).astype(jnp.bfloat16)


def attend(q_ref, q_start, kv, k_start, window, width, o_ref):
    rows = pl.ds(q_start, SPAN)
    keys = pl.ds(k_start, window)
    for h in range(width // HEAD_DIM):
        cols = slice(h * HEAD_DIM, (h + 1) * HEAD_DIM)
        vcols = slice(width + h * HEAD_DIM, width + (h + 1) * HEAD_DIM)
        s = lax.dot_general(
            q_ref[rows, cols],
            kv[keys, cols],
            (((1,), (1,)), ((), ())),
            preferred_element_type=jnp.float32,
        ) * (1.0 / math.sqrt(HEAD_DIM))
        e = jnp.exp(s - jnp.max(s, axis=-1, keepdims=True))
        w = (e * (1.0 / jnp.sum(e, axis=-1, keepdims=True))).astype(jnp.bfloat16)
        o_ref[rows, cols] = jnp.dot(
            w, kv[keys, vcols], preferred_element_type=jnp.float32
        ).astype(jnp.bfloat16)


def compute_kernel(g_ref, wk_ref, wv_ref, q_ref, o_ref, xs, kv):
    slices, rows, part = g_ref.shape
    width = wk_ref.shape[1]
    chunk_rows = xs.shape[0]
    window = chunk_rows // CHUNK_SPANS

    @pl.loop(0, rows // chunk_rows)
    def _(c):
        start = pl.multiple_of(c * chunk_rows, chunk_rows)
        for f in range(slices):
            xs[:, f * part : (f + 1) * part] = g_ref[f, pl.ds(start, chunk_rows), :]
        project(xs, wk_ref, wv_ref, kv)
        for j in range(CHUNK_SPANS):
            q_start = pl.multiple_of((c * CHUNK_SPANS + j) * SPAN, SPAN)
            attend(q_ref, q_start, kv, j * window, window, width, o_ref)


def fetch_blocks(encodings, nb_owner, nb_block):
    span_dev, neighbours = nb_owner.shape
    entries = span_dev * neighbours
    db_local, block_len, slice_width = encodings.shape
    peer_count = lax.axis_size("seq")
    slot_most = max(2, (entries + peer_count - 1) // peer_count)
    owner_ids = nb_owner.reshape(entries)
    block_ids = nb_block.reshape(entries)
    position = jnp.arange(entries, dtype=jnp.int32)
    same_owner = owner_ids[:, None] == owner_ids[None, :]
    before = position[None, :] < position[:, None]
    slot_ids = jnp.sum((same_owner & before).astype(jnp.int32), axis=1)
    owner_hit = owner_ids[:, None] == jnp.arange(peer_count, dtype=jnp.int32)[None, :]
    slot_hit = slot_ids[:, None] == jnp.arange(slot_most, dtype=jnp.int32)[None, :]
    marked = owner_hit[:, :, None] & slot_hit[:, None, :]
    requests = jnp.sum(jnp.where(marked, block_ids[:, None, None], 0), axis=0)
    asked_ids = lax.all_to_all(requests, "seq", split_axis=0, concat_axis=0, tiled=True)
    picked = jnp.take(encodings, asked_ids, axis=0)
    replies = lax.all_to_all(picked, "seq", split_axis=0, concat_axis=0, tiled=True)
    flat_rows = replies.reshape(peer_count * slot_most, block_len, slice_width)
    return jnp.take(flat_rows, owner_ids * slot_most + slot_ids, axis=0)


def on_device(queries, key_weight, value_weight, encodings, nb_owner, nb_block):
    span_dev, neighbours = nb_owner.shape
    token_count, width = queries.shape
    block_len, part = encodings.shape[1:]
    early = SPAN - 1
    ahead = moved(queries[:early], "seq", -1)
    lined = jnp.concatenate([queries[early:], ahead], axis=0)
    compact = fetch_blocks(encodings, nb_owner, nb_block)
    gathered = lax.all_gather(compact, "head", axis=0, tiled=False)
    gathered = gathered.reshape(gathered.shape[0], -1, part)
    chunk_rows = CHUNK_SPANS * neighbours * block_len
    vmem = pl.BlockSpec(memory_space=pltpu.VMEM)
    made = pl.pallas_call(
        compute_kernel,
        out_shape=jax.ShapeDtypeStruct((token_count, width), jnp.bfloat16),
        in_specs=[vmem] * 4,
        out_specs=vmem,
        scratch_shapes=[
            pltpu.VMEM((chunk_rows, gathered.shape[0] * part), jnp.bfloat16),
            pltpu.VMEM((chunk_rows, 2 * width), jnp.bfloat16),
        ],
        compiler_params=pltpu.CompilerParams(vmem_limit_bytes=48 << 20),
    )(gathered, key_weight, value_weight, lined)
    back = moved(made[token_count - early :], "seq", 1)
    return jnp.concatenate([back, made[: token_count - early]], axis=0)


def solution(mesh):
    return jax.shard_map(
        on_device,
        mesh=mesh,
        in_specs=(
            P("seq", "head"),
            P(None, "head"),
            P(None, "head"),
            P("seq", None, "head"),
            P("seq", None),
            P("seq", None),
        ),
        out_specs=P("seq", "head"),
        check_vma=False,
    )
```
